128 devices in a mesh: row: 32 (over z, x, core), col: 4 (over y).
Axes of the slice: x: 4, y: 4, z: 4, core: 2. Of those that a mesh axis runs over, the one named last changes fastest.
Arguments:
- state: float32 [2, 32768, 4096], P(None, 'row', 'col'), may hold values from -6 to 6
- panel: float32 [2, 32768, 2048], P(None, 'row', 'col'), may hold values from -1 to 1
- pivots: int32 [64], replicated, may hold values from 0 to 63, each once
Outputs:
- adjoint: float32 [2, 32768, 4096], P(None, 'row', 'col')
The draws below stay inside these ranges and needn't reach their ends.
Inputs may be any that keep to these rules, and one draw needn't show every extreme that they name: pivots names every block index once.
All inputs are finite; a program needn't handle non-finite values.
Results may differ from the reference program's by a relative error of at most 0.00007.
Values sent between devices are 32-bit elements; how exact they have to be, the bound alone decides.
A program may use at most 192 MiB of HBM per device.

```python
import math
import jax
import jax.numpy as jnp
from jax import lax

NB = 1024
KB_DEV = 2
R = 4096
KB = 64
ORDER = 65536
N_ROW = 32


def draw_panel(key, part):
    shape = (KB_DEV, N_ROW * NB, 2 * NB)
    spread = 1.0 / math.sqrt(ORDER // 8)
    noise = jax.random.normal(key, shape, jnp.float32) * spread
    slot_ids = jnp.arange(KB_DEV)[:, None, None]
    row_ids = jnp.arange(N_ROW * NB)[None, :, None]
    leading = jnp.logical_and(slot_ids == 0, row_ids < 2 * NB)
    values = noise + jnp.where(leading, 1.8 * spread, 0.0)
    limit = min(6.0 * spread, 1.0)
    return jnp.clip(values, -limit, limit).astype(jnp.float32)


def shard_levels(stream_key, shape, shards, low, largest):
    gain = 1.0
    for axis_at, parts in shards:
        draws = jax.random.uniform(jax.random.fold_in(jax.random.fold_in(stream_key, 6), axis_at), (parts,), jnp.float32, low / len(shards), largest / len(shards))
        gain = gain * jnp.repeat(jnp.exp(draws), shape[axis_at] // parts).reshape((-1,) + (1,) * (len(shape) - 1 - axis_at))
    return gain


def scatter_about(key, shape, width, most, split=(), held_as=jnp.bfloat16):
    result = jax.random.normal(key, shape, jnp.float32) * width
    if len(split) > 0:
        result = shard_levels(key, shape, split, -0.22, 0.18) * result
    return jnp.clip(result, min=-most, max=most).astype(held_as)


def setup_inputs(seed: int = 0) -> dict:
    streams_of = jax.random.split(jax.random.key(seed), 4)
    state = scatter_about(streams_of[0], (KB_DEV, N_ROW * NB, R), 1.0, 6.0, ((1, 32), (2, 4)), jnp.float32)
    panel = draw_panel(jax.random.fold_in(streams_of[3], 71), 0)
    pivots = jax.random.permutation(streams_of[2], KB).astype(jnp.int32)
    return dict(state=state, panel=panel, pivots=pivots)


def unit_solve(block, right):
    lower = jnp.tril(block, -1) + jnp.eye(block.shape[0], dtype=block.dtype)
    return lax.linalg.triangular_solve(lower, right, left_side=True, lower=True, transpose_a=True, unit_diagonal=True)

def reference(state, panel, pivots):
    count = KB_DEV * N_ROW
    field = state.reshape(count, NB, R)
    columns = panel.reshape(count, NB, 2 * NB)
    index = jnp.arange(count)

    def contract(part, values, lowest):
        weight = (index >= lowest).astype(jnp.float32)[:, None, None]
        return jnp.einsum('bic,bir->cr', part, values * weight, precision=lax.Precision.HIGHEST)
    upper_sum = contract(columns[:, :, NB:], field, 2)
    solved_one = unit_solve(columns[1, :, NB:], field[1] - upper_sum)
    field = field.at[1].set(solved_one)
    lower_sum = contract(columns[:, :, :NB], field, 1)
    solved_zero = unit_solve(columns[0, :, :NB], field[0] - lower_sum)
    field = field.at[0].set(solved_zero)
    permuted = jnp.take(field, pivots.astype(jnp.int32), axis=0)
    return permuted.reshape(KB_DEV, N_ROW * NB, R)
```

```python
import functools

import jax
import jax.numpy as jnp
from jax import lax
from jax.experimental import pallas as pl
from jax.experimental.pallas import tpu as pltpu
from jax.sharding import PartitionSpec as P

MESH = pl.DeviceIdType.MESH
F32 = jnp.float32
BF16 = jnp.bfloat16
DMA = pltpu.SemaphoreType.DMA

ORDER = (20, 21, 1, 12, 24, 13, 25, 18, 6, 19, 7, 22, 2, 23, 3, 28, 8, 29, 9, 4, 16, 5, 17, 10, 30, 11, 31, 14, 26, 15, 27)


def split(v):
    hi = v.astype(BF16)
    return hi, (v - hi.astype(F32)).astype(BF16)


def dot_high(a, b):
    return jnp.dot(a, b, precision=lax.Precision.HIGHEST, preferred_element_type=F32)


def inverse_unit_lower(low):
    rows = lax.broadcasted_iota(jnp.int32, (128, 128), 0)
    cols = lax.broadcasted_iota(jnp.int32, (128, 128), 1)

    def part(s):
        keep = (rows // (2 * s) == cols // (2 * s)) & ((rows // s) % 2 == 1) & ((cols // s) % 2 == 0)
        return jnp.where(keep, low, 0.0)

    inv = jnp.where(rows == cols, 1.0, 0.0) - part(1)
    for s in (2, 4, 8, 16, 32, 64):
        inv = inv - dot_high(dot_high(inv, part(s)), inv)
    return inv


def main_kernel(
    state, panel, piv, out, z1t, z0t, gath, ufull,
    zst, zhi, zlo, cst, chi, clo, st, xc, bx, bz, cx, cz, first, second, upc, dinv, dblk, rt, sol, rhs, u0,
    ysend, yrecv, asend, arecv, usend, urecv, rsend, rrecv, gsend, grecv, local,
):
    p = lax.axis_index("row")
    y = lax.axis_index("col")
    z, x, c = p // 8, (p // 2) % 4, p % 2

    def row_of(zz, xx, cc):
        return ((zz % 4) * 4 + xx % 4) * 2 + cc

    def peer(k):
        return row_of(z + k // 8, x + (k // 2) % 4, (c + k % 2) % 2)

    sibling = row_of(z, x, 1 - c)

    def rcopy(src, dst, ss, rs, row, col):
        return pltpu.make_async_remote_copy(src, dst, ss, rs, device_id=(row, col), device_id_type=MESH)

    def wait_recv(ref, rs):
        rcopy(ref, ref, rs, rs, sibling, y).wait_recv()

    def wait_send(ref, ss):
        rcopy(ref, ref, ss, ss, sibling, y).wait_send()

    right, left, across = (y + 1) % 4, (y + 3) % 4, (y + 2) % 4

    barrier = pltpu.get_barrier_semaphore()
    for k in range(1, 32):
        pl.semaphore_signal(barrier, inc=1, device_id=(peer(k), y), device_id_type=MESH)
    for d in (right, left, across):
        pl.semaphore_signal(barrier, inc=1, device_id=(p, d), device_id_type=MESH)
    pl.semaphore_wait(barrier, 34)

    y_own = [
        rcopy(panel.at[0], gath.at[3, 0], ysend.at[0], yrecv.at[0], p, right),
        rcopy(panel.at[1], gath.at[1, 1], ysend.at[1], yrecv.at[1], p, left),
        rcopy(panel.at[1], gath.at[3, 1], ysend.at[2], yrecv.at[2], p, right),
        rcopy(panel.at[0], gath.at[1, 0], ysend.at[3], yrecv.at[3], p, left),
    ]
    y_fwd = [
        rcopy(gath.at[3, 0], gath.at[2, 0], ysend.at[4], yrecv.at[4], p, right),
        rcopy(gath.at[1, 1], gath.at[2, 1], ysend.at[5], yrecv.at[5], p, left),
    ]

    lane1 = pl.ds(pl.multiple_of(y * 512, 512), 512)
    lane0 = pl.ds(pl.multiple_of(2048 + (y % 2) * 512, 512), 512)

    def scatter(lanes, sem):
        for k in range(1, 32):
            q = peer(k)
            rows = pl.ds(pl.multiple_of(q * 32, 32), 32)
            rcopy(panel.at[0, rows], upc.at[:, lanes], usend.at[sem], urecv.at[sem], q, y).start()
        rows = pl.ds(pl.multiple_of(p * 32, 32), 32)
        pltpu.make_async_copy(panel.at[0, rows], upc.at[:, lanes], urecv.at[sem]).start()

    def scatter_done(sem):
        wait_send(panel.at[0, pl.ds(0, 31 * 32)], usend.at[sem])

    def u_round_y():
        wait_recv(upc.at[:, pl.ds(0, 512)], urecv.at[0])
        for d in (right, left, across):
            rcopy(upc.at[:, lane1], upc.at[:, lane1], usend.at[2], urecv.at[2], p, d).start()

        @pl.when(y < 2)
        def _():
            wait_recv(upc.at[:, pl.ds(0, 512)], urecv.at[1])
            for d in (right, left, across):
                rcopy(upc.at[:, lane0], upc.at[:, lane0], usend.at[3], urecv.at[3], p, d).start()

    def u_here():
        wait_recv(upc.at[:, pl.ds(0, 1536)], urecv.at[2])

        @pl.when(y < 2)
        def _():
            wait_recv(upc.at[:, pl.ds(0, 512)], urecv.at[3])

        @pl.when(y >= 2)
        def _():
            wait_recv(upc.at[:, pl.ds(0, 1024)], urecv.at[3])

    def gather_a(share, full, h, base):
        pltpu.make_async_copy(share, full.at[z, x, c], local.at[10 + base // 5]).start()
        for d in (1, 3, 2):
            rcopy(share.at[:, pl.ds(0, h)], full.at[z, x, c, :, pl.ds(0, h)], gsend.at[base], grecv.at[base],
                  row_of(z, x + d, c), y).start()
            rcopy(share.at[:, pl.ds(h, h)], full.at[z, x, c, :, pl.ds(h, h)], gsend.at[base + 1], grecv.at[base + 1],
                  row_of(z + d, x, c), y).start()

    def gather_b(share, full, h, base):
        pltpu.make_async_copy(share, full.at[z, x, c], local.at[10 + base // 5]).wait()
        wait_recv(full.at[0, pl.ds(0, 3), 0, :, pl.ds(0, h)], grecv.at[base])
        for d in (1, 3, 2):
            here = full.at[z, :, c, :, pl.ds(0, h)]
            rcopy(here, here, gsend.at[base + 2], grecv.at[base + 2], row_of(z + d, x, c), y).start()
        wait_recv(full.at[0, pl.ds(0, 3), 0, :, pl.ds(0, h)], grecv.at[base + 1])
        for d in (1, 3, 2):
            here = full.at[:, x, c, :, pl.ds(h, h)]
            rcopy(here, here, gsend.at[base + 3], grecv.at[base + 3], row_of(z, x + d, c), y).start()

    def gather_c(full, h, base):
        wait_recv(full.at[pl.ds(0, 3), :, 0, :, pl.ds(0, h)], grecv.at[base + 2])
        wait_recv(full.at[pl.ds(0, 3), :, 0, :, pl.ds(0, h)], grecv.at[base + 3])
        rcopy(full.at[:, :, c], full.at[:, :, c], gsend.at[base + 4], grecv.at[base + 4], sibling, y).start()

    def gather_end(full, base):
        wait_recv(full.at[:, :, 0], grecv.at[base + 4])

    def gather_sent(full, h, base):
        for i in (0, 1):
            wait_send(full.at[0, pl.ds(0, 3), 0, :, pl.ds(0, h)], gsend.at[base + i])
        for i in (2, 3):
            wait_send(full.at[pl.ds(0, 3), :, 0, :, pl.ds(0, h)], gsend.at[base + i])
        wait_send(full.at[:, :, 0], gsend.at[base + 4])

    def first_sends(lo, hi):
        for k in ORDER[lo:hi]:
            q = peer(k)
            rows = pl.ds(pl.multiple_of(q * 32, 32), 32)
            rcopy(state.at[:, rows], first.at[z, x, c], asend.at[0], arecv.at[0], q, y).start()

    my_rows = pl.ds(pl.multiple_of(p * 32, 32), 32)

    def second_sends(lo, hi):
        for k in ORDER[lo:hi]:
            q = peer(k)
            rcopy(second.at[q], out.at[:, my_rows], asend.at[1], arecv.at[1], q, y).start()

    def reorder():
        @pl.loop(0, 32)
        def _(q):
            for slot in range(2):
                b = piv[slot * 32 + q]
                owner = b % 32
                second[q, slot] = first[owner // 8, (owner // 2) % 4, owner % 2, b // 32]

    def transposed(slot, part, buf):
        pltpu.make_async_copy(
            state.at[slot, pl.ds(part * 256, 256)], zst.at[buf], local.at[buf]).wait()

        @pl.loop(0, 4)
        def _(j):
            rows = pl.ds(pl.multiple_of(j * 256, 256), 256)
            hi, lo = split(zst[buf, :, rows].T)
            zhi[slot, rows, part * 256:part * 256 + 256] = hi
            zlo[slot, rows, part * 256:part * 256 + 256] = lo

    def load_state(slot, part, buf):
        pltpu.make_async_copy(
            state.at[slot, pl.ds(part * 256, 256)], zst.at[buf], local.at[buf]).start()

    def load_panel(src, buf):
        pltpu.make_async_copy(src, cst.at[buf], local.at[3 + buf]).start()

    keep = jnp.where(p >= 2, 1.0, 0.0).astype(F32)

    def product(k, slot, buf, new):
        pltpu.make_async_copy(panel.at[0], cst.at[buf], local.at[3 + buf]).wait()
        q = (y + k) % 4
        mark = jnp.where(((p == 0) & (q < 2)) | ((p == 1) & (q >= 2)), -1.0, 0.0).astype(F32)

        @pl.loop(0, 8)
        def _(i):
            rows = pl.ds(pl.multiple_of(i * 128, 128), 128)
            v = cst[buf, rows]
            if slot == 0:
                rr = lax.broadcasted_iota(jnp.int32, (128, 512), 0) + i * 128
                cc = lax.broadcasted_iota(jnp.int32, (128, 512), 1) + (q % 2) * 512
                v = v * keep + jnp.where(rr == cc, mark, 0.0)
            hi, lo = split(v)
            chi[rows] = hi
            clo[rows] = lo

        @pl.loop(0, 4)
        def _(j):
            rows = pl.ds(pl.multiple_of(j * 256, 256), 256)
            a_hi, a_lo = zhi[slot, rows], zlo[slot, rows]
            b_hi = chi[...]
            acc = jnp.dot(a_hi, b_hi, preferred_element_type=F32)
            acc += jnp.dot(a_hi, clo[...], preferred_element_type=F32)
            acc += jnp.dot(a_lo, b_hi, preferred_element_type=F32)
            acc = acc.reshape(4, 2, 32, 512)
            if new:
                st[k, j] = acc
            else:
                st[k, j] = st[k, j] + acc

    def rs_core(k):
        rcopy(st.at[k, :, :, 1 - c], xc.at[k], rsend.at[5 * k], rrecv.at[5 * k], sibling, y).start()

    def rs_one(k):
        wait_recv(xc.at[k], rrecv.at[5 * k])

        @pl.loop(0, 16)
        def _(i):
            xc[k, i // 4, i % 4] = xc[k, i // 4, i % 4] + st[k, i // 4, i % 4, c]

        for d in (1, 3, 2):
            rcopy(xc.at[k, :, (x + d) % 4, :, pl.ds(0, 256)], bx.at[k, d - 1], rsend.at[5 * k + 1],
                  rrecv.at[5 * k + 1], row_of(z, x + d, c), y).start()
            rcopy(xc.at[k, (z + d) % 4, :, :, pl.ds(256, 256)], bz.at[k, d - 1], rsend.at[5 * k + 2],
                  rrecv.at[5 * k + 2], row_of(z + d, x, c), y).start()

    def rs_two(k):
        wait_recv(bx.at[k], rrecv.at[5 * k + 1])
        for i in range(4):
            bx[k, 0, i] = bx[k, 0, i] + bx[k, 1, i] + bx[k, 2, i] + xc[k, i, x, :, 0:256]
        for d in (1, 3, 2):
            rcopy(bx.at[k, 0, (z + d) % 4], cx.at[k, d - 1], rsend.at[5 * k + 3], rrecv.at[5 * k + 3],
                  row_of(z + d, x, c), y).start()
        wait_recv(bz.at[k], rrecv.at[5 * k + 2])
        for i in range(4):
            bz[k, 0, i] = bz[k, 0, i] + bz[k, 1, i] + bz[k, 2, i] + xc[k, z, i, :, 256:512]
        for d in (1, 3, 2):
            rcopy(bz.at[k, 0, (x + d) % 4], cz.at[k, d - 1], rsend.at[5 * k + 4], rrecv.at[5 * k + 4],
                  row_of(z, x + d, c), y).start()

    def rs_three(k):
        q = (y + k) % 4
        wait_recv(cx.at[k], rrecv.at[5 * k + 3])
        rt[q, :, 0:256] = bx[k, 0, z] + cx[k, 0] + cx[k, 1] + cx[k, 2]
        wait_recv(cz.at[k], rrecv.at[5 * k + 4])
        rt[q, :, 256:512] = bz[k, 0, x] + cz[k, 0] + cz[k, 1] + cz[k, 2]

    def rs_sent(k):
        wait_send(xc.at[k], rsend.at[5 * k])
        wait_send(bx.at[k], rsend.at[5 * k + 1])
        wait_send(bz.at[k], rsend.at[5 * k + 2])
        wait_send(cx.at[k], rsend.at[5 * k + 3])
        wait_send(cz.at[k], rsend.at[5 * k + 4])

    def blocks_in():
        for j in range(8):
            rows = (j // 2, pl.ds((j % 2) * 2, 2))
            pltpu.make_async_copy(
                ufull.at[rows[0], rows[1], :, :, pl.ds(1024 + 128 * j, 128)], dblk.at[j], local.at[5]).start()
            pltpu.make_async_copy(
                ufull.at[rows[0], rows[1], :, :, pl.ds(2048 + 128 * j, 128)], dblk.at[8 + j], local.at[5]).start()
        pltpu.make_async_copy(dblk, dblk, local.at[5]).wait()

    def inverses():
        @pl.loop(0, 4)
        def _(g):
            for i in range(4):
                dinv[g * 4 + i] = inverse_unit_lower(dblk[g * 4 + i].reshape(128, 128))

    def u_copies():
        return [
            pltpu.make_async_copy(ufull.at[:, :, :, :, pl.ds(1024, 1024)], first.at[:, :, :, 0], local.at[6]),
            pltpu.make_async_copy(ufull.at[:, :, :, :, pl.ds(0, 1024)], first.at[:, :, :, 1], local.at[7]),
            pltpu.make_async_copy(ufull.at[:, :, :, :, pl.ds(2048, 1024)], u0, local.at[8]),
        ]

    def substitute(base, upper):
        for j in range(7, -1, -1):
            xj = dot_high(rhs[:, 128 * j:128 * j + 128], dinv[base + j])
            sol[base // 8, :, 128 * j:128 * j + 128] = xj
            if j:
                rhs[:, 0:128 * j] = rhs[:, 0:128 * j] - dot_high(xj, upper(j))

    y_own[0].start()
    y_own[1].start()

    @pl.when(p == 1)
    def _():
        scatter(lane1, 0)

    @pl.when((p == 0) & (y < 2))
    def _():
        scatter(lane0, 1)

    pltpu.make_async_copy(state.at[:, my_rows], first.at[z, x, c], local.at[9]).start()
    first_sends(0, 8)

    load_state(0, 0, 0)
    load_panel(panel.at[0], 0)
    load_panel(panel.at[1], 1)
    for t in range(8):
        if t < 7:
            load_state((t + 1) // 4, (t + 1) % 4, (t + 1) % 2)
        transposed(t // 4, t % 4, t % 2)
    product(0, 0, 0, True)
    u_round_y()
    y_own[2].start()
    y_own[3].start()
    first_sends(8, 12)
    product(0, 1, 1, False)
    rs_core(0)
    rs_one(0)
    first_sends(12, 16)

    y_own[0].wait_recv()
    y_fwd[0].start()
    load_panel(gath.at[3, 0], 0)
    y_own[1].wait_recv()
    y_fwd[1].start()
    load_panel(gath.at[1, 1], 1)
    product(3, 0, 0, True)
    u_here()
    gather_a(upc, ufull, 1536, 0)
    first_sends(16, 21)
    product(1, 1, 1, True)
    rs_two(0)
    gather_b(upc, ufull, 1536, 0)
    first_sends(21, 31)
    rs_three(0)

    y_own[2].wait_recv()
    load_panel(gath.at[3, 1], 0)
    y_own[3].wait_recv()
    load_panel(gath.at[1, 0], 1)
    product(3, 1, 0, False)
    rs_core(3)
    product(1, 0, 1, False)
    rs_core(1)
    gather_c(ufull, 1536, 0)
    rs_one(3)
    rs_one(1)
    gather_end(ufull, 0)
    blocks_in()
    inverses()

    pltpu.make_async_copy(state.at[:, my_rows], first.at[z, x, c], local.at[9]).wait()
    wait_recv(second.at[pl.ds(0, 31)], arecv.at[0])
    reorder()
    pltpu.make_async_copy(second.at[p], out.at[:, my_rows], local.at[9]).start()
    second_sends(0, 5)
    rs_two(3)
    rs_two(1)
    uc = u_copies()
    for copy in uc:
        copy.start()

    y_fwd[0].wait_recv()
    load_panel(gath.at[2, 0], 0)
    y_fwd[1].wait_recv()
    load_panel(gath.at[2, 1], 1)
    product(2, 0, 0, True)
    product(2, 1, 1, False)
    rs_core(2)
    second_sends(5, 10)
    rs_one(2)
    second_sends(10, 15)
    rs_three(3)
    rs_three(1)
    rs_two(2)
    second_sends(15, 20)
    rs_three(2)


    def row_block(j, slot, lanes):
        return first[j // 2, (j % 2) * 2:(j % 2) * 2 + 2, :, slot, :, 0:lanes].reshape(128, lanes)

    rhs[:, 0:512] = -rt[2]
    rhs[:, 512:1024] = -rt[3]
    uc[0].wait()
    substitute(0, lambda j: row_block(j, 0, 128 * j))
    gather_a(sol.at[0], z1t, 512, 5)
    second_sends(20, 24)
    rhs[:, 0:512] = -rt[0]
    rhs[:, 512:1024] = -rt[1]
    uc[1].wait()
    for j in range(8):
        rhs[...] = rhs[...] - dot_high(sol[0, :, 128 * j:128 * j + 128], row_block(j, 1, 1024))
    uc[2].wait()
    substitute(8, lambda j: u0[j // 2, (j % 2) * 2:(j % 2) * 2 + 2, :, :, 0:128 * j].reshape(128, 128 * j))
    gather_b(sol.at[0], z1t, 512, 5)
    gather_a(sol.at[1], z0t, 512, 10)
    second_sends(24, 31)
    gather_c(z1t, 512, 5)
    gather_b(sol.at[1], z0t, 512, 10)
    gather_c(z0t, 512, 10)
    gather_end(z1t, 5)
    gather_end(z0t, 10)
    wait_recv(second.at[pl.ds(0, 31)], arecv.at[1])
    pltpu.make_async_copy(second.at[p], out.at[:, my_rows], local.at[9]).wait()

    for d in y_own + y_fwd:
        d.wait_send()

    @pl.when(p == 1)
    def _():
        scatter_done(0)

    @pl.when((p == 0) & (y < 2))
    def _():
        scatter_done(1)

    wait_send(upc.at[:, pl.ds(0, 1536)], usend.at[2])

    @pl.when(y < 2)
    def _():
        wait_send(upc.at[:, pl.ds(0, 1536)], usend.at[3])

    for i in range(2):
        wait_send(second.at[pl.ds(0, 31)], asend.at[i])
    for k in range(4):
        rs_sent(k)
    gather_sent(ufull, 1536, 0)
    gather_sent(z1t, 512, 5)
    gather_sent(z0t, 512, 10)


def main_call(state, panel, pivots):
    any_spec = pl.BlockSpec(memory_space=pl.ANY)
    shape = jax.ShapeDtypeStruct
    outs = [
        shape((2, 1024, 1024), F32), shape((4, 4, 2, 32, 1024), F32), shape((4, 4, 2, 32, 1024), F32),
        shape((4, 2, 1024, 512), F32), shape((4, 4, 2, 32, 3072), F32),
    ]
    vmem = [
        ((2, 256, 1024), F32), ((2, 1024, 1024), BF16), ((2, 1024, 1024), BF16), ((2, 1024, 512), F32),
        ((1024, 512), BF16), ((1024, 512), BF16), ((4, 4, 4, 2, 32, 512), F32), ((4, 4, 4, 32, 512), F32),
        ((4, 3, 4, 32, 256), F32), ((4, 3, 4, 32, 256), F32), ((4, 3, 32, 256), F32), ((4, 3, 32, 256), F32),
        ((4, 4, 2, 2, 32, 1024), F32), ((32, 2, 32, 1024), F32), ((32, 3072), F32), ((16, 128, 128), F32),
        ((16, 2, 2, 32, 128), F32), ((4, 32, 512), F32), ((2, 32, 1024), F32), ((32, 1024), F32),
        ((4, 4, 2, 32, 1024), F32),
    ]
    sems = [6, 6, 2, 2, 4, 4, 20, 20, 15, 15, 13]
    return pl.pallas_call(
        main_kernel,
        out_shape=outs,
        in_specs=[any_spec, any_spec, pl.BlockSpec(memory_space=pltpu.SMEM)],
        out_specs=[any_spec] * 5,
        scratch_shapes=[pltpu.VMEM(*v) for v in vmem] + [DMA((n,)) for n in sems],
        compiler_params=pltpu.CompilerParams(
            collective_id=0, has_side_effects=True, vmem_limit_bytes=60 << 20),
    )(state, panel, pivots)


def select_kernel(ids, moved, z1, z0, out):
    block = ids[pl.program_id(0)]

    @pl.when(block >= 2)
    def _():
        out[0] = moved[0]

    @pl.when(block == 1)
    def _():
        out[0] = z1[...].T

    @pl.when(block == 0)
    def _():
        out[0] = z0[...].T


def select_call(ids, moved, z1, z0):
    tile = 128

    def solved(which):
        return pl.BlockSpec((1024, tile), lambda l, i, ids: (0, jnp.where(ids[l] == which, i, 0)))

    return pl.pallas_call(
        select_kernel,
        out_shape=jax.ShapeDtypeStruct((2, 1024, 1024), F32),
        grid_spec=pltpu.PrefetchScalarGridSpec(
            num_scalar_prefetch=1, grid=(2, 1024 // tile),
            in_specs=[pl.BlockSpec((1, tile, 1024), lambda l, i, ids: (l, i, 0)), solved(1), solved(0)],
            out_specs=pl.BlockSpec((1, tile, 1024), lambda l, i, ids: (l, i, 0))),
    )(ids, moved, z1, z0)


def body(state, panel, pivots):
    ids = lax.dynamic_slice(pivots.reshape(2, 32), (0, lax.axis_index("row")), (2, 1)).reshape(2)
    moved, z1t, z0t, _, _ = main_call(state, panel, pivots)
    return select_call(ids, moved, z1t.reshape(1024, 1024), z0t.reshape(1024, 1024))


def solution(mesh):
    placed = (P(None, "row", "col"), P(None, "row", "col"), P())
    return jax.shard_map(
        body, mesh=mesh, in_specs=placed, out_specs=P(None, "row", "col"), check_vma=False)
```

```python
import functools

import jax
import jax.numpy as jnp
from jax import lax
from jax.experimental import pallas as pl
from jax.experimental.pallas import tpu as pltpu
from jax.sharding import PartitionSpec as P

MESH = pl.DeviceIdType.MESH
F32 = jnp.float32
BF16 = jnp.bfloat16
DMA = pltpu.SemaphoreType.DMA

ORDER = (20, 21, 1, 12, 24, 13, 25, 18, 6, 19, 7, 22, 2, 23, 3, 28, 8, 29, 9, 4, 16, 5, 17, 10, 30, 11, 31, 14, 26, 15, 27)


def split(v):
    hi = v.astype(BF16)
    return hi, (v - hi.astype(F32)).astype(BF16)


def dot_high(a, b):
    return jnp.dot(a, b, precision=lax.Precision.HIGHEST, preferred_element_type=F32)


def inverse_unit_lower(low):
    rows = lax.broadcasted_iota(jnp.int32, (128, 128), 0)
    cols = lax.broadcasted_iota(jnp.int32, (128, 128), 1)

    def part(s):
        keep = (rows // (2 * s) == cols // (2 * s)) & ((rows // s) % 2 == 1) & ((cols // s) % 2 == 0)
        return jnp.where(keep, low, 0.0)

    inv = jnp.where(rows == cols, 1.0, 0.0) - part(1)
    for s in (2, 4, 8, 16, 32, 64):
        inv = inv - dot_high(dot_high(inv, part(s)), inv)
    return inv


def main_kernel(
    state, panel, piv, out, solved, gath, ufull,
    zst, zhi, zlo, cst, chi, clo, st, xc, bx, bz, cx, cz, first, second, upc, packed, dinv, dblk, rt, sol, rhs,
    ysend, yrecv, asend, arecv, usend, urecv, rsend, rrecv, gsend, grecv, local,
):
    p = lax.axis_index("row")
    y = lax.axis_index("col")
    z, x, c = p // 8, (p // 2) % 4, p % 2

    def row_of(zz, xx, cc):
        return ((zz % 4) * 4 + xx % 4) * 2 + cc

    def peer(k):
        return row_of(z + k // 8, x + (k // 2) % 4, (c + k % 2) % 2)

    sibling = row_of(z, x, 1 - c)

    def rcopy(src, dst, ss, rs, row, col):
        return pltpu.make_async_remote_copy(src, dst, ss, rs, device_id=(row, col), device_id_type=MESH)

    def wait_recv(ref, rs):
        rcopy(ref, ref, rs, rs, sibling, y).wait_recv()

    def wait_send(ref, ss):
        rcopy(ref, ref, ss, ss, sibling, y).wait_send()

    right, left, across = (y + 1) % 4, (y + 3) % 4, (y + 2) % 4

    barrier = pltpu.get_barrier_semaphore()
    for k in range(1, 32):
        pl.semaphore_signal(barrier, inc=1, device_id=(peer(k), y), device_id_type=MESH)
    for d in (right, left, across):
        pl.semaphore_signal(barrier, inc=1, device_id=(p, d), device_id_type=MESH)
    pl.semaphore_wait(barrier, 34)

    top, bottom = pl.ds(0, 512), pl.ds(512, 512)
    y_own = [
        rcopy(panel.at[0, top], gath.at[3, 0, top], ysend.at[0], yrecv.at[0], p, right),
        rcopy(panel.at[1, top], gath.at[1, 1, top], ysend.at[1], yrecv.at[1], p, left),
        rcopy(panel.at[0, bottom], gath.at[3, 0, bottom], ysend.at[2], yrecv.at[2], p, right),
        rcopy(panel.at[1, bottom], gath.at[1, 1, bottom], ysend.at[3], yrecv.at[3], p, left),
        rcopy(panel.at[1], gath.at[3, 1], ysend.at[4], yrecv.at[4], p, right),
        rcopy(panel.at[0], gath.at[1, 0], ysend.at[5], yrecv.at[5], p, left),
    ]
    y_fwd = [
        rcopy(gath.at[3, 0], gath.at[2, 0], ysend.at[6], yrecv.at[6], p, right),
        rcopy(gath.at[1, 1], gath.at[2, 1], ysend.at[7], yrecv.at[7], p, left),
    ]

    lane1 = pl.ds(pl.multiple_of(y * 512, 512), 512)
    lane0 = pl.ds(pl.multiple_of(2048 + (y % 2) * 512, 512), 512)

    def scatter(lanes, sem):
        def rows_for(q):
            return pl.ds(pl.multiple_of((q if sem == 0 else 31 - q) * 32, 32), 32)

        for k in ORDER:
            q = peer(k)
            rcopy(panel.at[0, rows_for(q)], upc.at[:, lanes], usend.at[sem], urecv.at[sem], q, y).start()
        pltpu.make_async_copy(panel.at[0, rows_for(p)], upc.at[:, lanes], urecv.at[sem]).start()

    def scatter_done(sem):
        wait_send(panel.at[0, pl.ds(0, 31 * 32)], usend.at[sem])

    def u_round_y():
        wait_recv(upc.at[:, pl.ds(0, 512)], urecv.at[0])
        for d in (right, left, across):
            rcopy(upc.at[:, lane1], upc.at[:, lane1], usend.at[2], urecv.at[2], p, d).start()

        @pl.when(y < 2)
        def _():
            wait_recv(upc.at[:, pl.ds(0, 512)], urecv.at[1])
            for d in (right, left, across):
                rcopy(upc.at[:, lane0], upc.at[:, lane0], usend.at[3], urecv.at[3], p, d).start()

    def u_here():
        wait_recv(upc.at[:, pl.ds(0, 1536)], urecv.at[2])

        @pl.when(y < 2)
        def _():
            wait_recv(upc.at[:, pl.ds(0, 512)], urecv.at[3])

        @pl.when(y >= 2)
        def _():
            wait_recv(upc.at[:, pl.ds(0, 1024)], urecv.at[3])

    def u_pack():
        g = p // 4
        for t in range(9):
            lane = jnp.where(t <= g, 1024 + 128 * t, 2048 + 128 * (t - g - 1))
            packed[:, 128 * t:128 * t + 128] = upc[:, pl.ds(pl.multiple_of(lane, 128), 128)]
        packed[:, 1152:2176] = upc[:, 0:1024]

    def gather_a(share, full, h, w, base):
        pltpu.make_async_copy(share, full.at[z, x, c], local.at[10 + base // 5]).start()
        for d in (1, 3, 2):
            rcopy(share.at[:, pl.ds(0, h)], full.at[z, x, c, :, pl.ds(0, h)], gsend.at[base], grecv.at[base],
                  row_of(z, x + d, c), y).start()
            rcopy(share.at[:, pl.ds(h, w - h)], full.at[z, x, c, :, pl.ds(h, w - h)], gsend.at[base + 1],
                  grecv.at[base + 1], row_of(z + d, x, c), y).start()

    def gather_b(share, full, h, w, base):
        pltpu.make_async_copy(share, full.at[z, x, c], local.at[10 + base // 5]).wait()
        wait_recv(full.at[0, pl.ds(0, 3), 0, :, pl.ds(0, h)], grecv.at[base])
        for d in (1, 3, 2):
            here = full.at[z, :, c, :, pl.ds(0, h)]
            rcopy(here, here, gsend.at[base + 2], grecv.at[base + 2], row_of(z + d, x, c), y).start()
        wait_recv(full.at[0, pl.ds(0, 3), 0, :, pl.ds(h, w - h)], grecv.at[base + 1])
        for d in (1, 3, 2):
            here = full.at[:, x, c, :, pl.ds(h, w - h)]
            rcopy(here, here, gsend.at[base + 3], grecv.at[base + 3], row_of(z, x + d, c), y).start()

    def gather_c(full, h, w, base):
        wait_recv(full.at[pl.ds(0, 3), :, 0, :, pl.ds(0, h)], grecv.at[base + 2])
        wait_recv(full.at[pl.ds(0, 3), :, 0, :, pl.ds(h, w - h)], grecv.at[base + 3])
        rcopy(full.at[:, :, c], full.at[:, :, c], gsend.at[base + 4], grecv.at[base + 4], sibling, y).start()

    def gather_end(full, base):
        wait_recv(full.at[:, :, 0], grecv.at[base + 4])

    def gather_sent(full, h, w, base):
        wait_send(full.at[0, pl.ds(0, 3), 0, :, pl.ds(0, h)], gsend.at[base])
        wait_send(full.at[0, pl.ds(0, 3), 0, :, pl.ds(h, w - h)], gsend.at[base + 1])
        wait_send(full.at[pl.ds(0, 3), :, 0, :, pl.ds(0, h)], gsend.at[base + 2])
        wait_send(full.at[pl.ds(0, 3), :, 0, :, pl.ds(h, w - h)], gsend.at[base + 3])
        wait_send(full.at[:, :, 0], gsend.at[base + 4])

    def rows_of(q):
        return pl.ds(pl.multiple_of(q * 32, 32), 32)

    def first_sends(lo, hi):
        @pl.when(p >= 2)
        def _():
            for k in ORDER[lo:hi]:
                q = peer(k)
                rcopy(state.at[:, rows_of(q)], first.at[z, x, c], asend.at[0], arecv.at[0], q, y).start()

        @pl.when(p < 2)
        def _():
            for k in ORDER[lo:hi]:
                q = peer(k)
                rcopy(state.at[1, rows_of(q)], first.at[z, x, c, 1], asend.at[0], arecv.at[0], q, y).start()

    def first_own():
        first[0, 0, 0, 0] = jnp.zeros((32, 1024), F32)
        first[0, 0, 1, 0] = jnp.zeros((32, 1024), F32)

        @pl.when(p >= 2)
        def _():
            pltpu.make_async_copy(state.at[0, rows_of(p)], first.at[z, x, c, 0], local.at[9]).start()
            pltpu.make_async_copy(state.at[0, rows_of(p)], first.at[z, x, c, 0], local.at[9]).wait()

        pltpu.make_async_copy(state.at[1, rows_of(p)], first.at[z, x, c, 1], local.at[9]).start()
        pltpu.make_async_copy(state.at[1, rows_of(p)], first.at[z, x, c, 1], local.at[9]).wait()

    def first_here():
        @pl.when(p >= 2)
        def _():
            wait_recv(second.at[pl.ds(0, 30)], arecv.at[0])

        @pl.when(p < 2)
        def _():
            wait_recv(state.at[:, pl.ds(0, 976)], arecv.at[0])

    def first_sent():
        @pl.when(p >= 2)
        def _():
            wait_send(second.at[pl.ds(0, 31)], asend.at[0])

        @pl.when(p < 2)
        def _():
            wait_send(state.at[0, pl.ds(0, 992)], asend.at[0])

    my_rows = pl.ds(pl.multiple_of(p * 32, 32), 32)

    def second_sends(lo, hi):
        for k in ORDER[lo:hi]:
            q = peer(k)
            rcopy(second.at[q], out.at[:, my_rows], asend.at[1], arecv.at[1], q, y).start()

    def reorder():
        @pl.loop(0, 32)
        def _(q):
            for slot in range(2):
                b = piv[slot * 32 + q]
                owner = b % 32
                second[q, slot] = first[owner // 8, (owner // 2) % 4, owner % 2, b // 32]

    def transposed(slot, part, buf):
        pltpu.make_async_copy(
            state.at[slot, pl.ds(part * 256, 256)], zst.at[buf], local.at[buf]).wait()
        transposed_body(slot, part, buf)

    def transposed_body(slot, part, buf):
        @pl.loop(0, 4)
        def _(j):
            rows = pl.ds(pl.multiple_of(j * 256, 256), 256)
            hi, lo = split(zst[buf, :, rows].T)
            zhi[slot, rows, part * 256:part * 256 + 256] = hi
            zlo[slot, rows, part * 256:part * 256 + 256] = lo

    def load_state(slot, part, buf):
        pltpu.make_async_copy(
            state.at[slot, pl.ds(part * 256, 256)], zst.at[buf], local.at[buf]).start()

    def load_panel(src, buf):
        pltpu.make_async_copy(src, cst.at[buf], local.at[3 + buf]).start()

    keep = jnp.where(p >= 2, 1.0, 0.0).astype(F32)

    def product(k, slot, buf, new):
        pltpu.make_async_copy(panel.at[0], cst.at[buf], local.at[3 + buf]).wait()
        product_body(k, slot, buf, new)

    def product_body(k, slot, buf, new):
        q = (y + k) % 4
        mark = jnp.where(((p == 0) & (q < 2)) | ((p == 1) & (q >= 2)), -1.0, 0.0).astype(F32)

        @pl.loop(0, 8)
        def _(i):
            rows = pl.ds(pl.multiple_of(i * 128, 128), 128)
            v = cst[buf, rows]
            if slot == 0:
                rr = lax.broadcasted_iota(jnp.int32, (128, 512), 0) + i * 128
                cc = lax.broadcasted_iota(jnp.int32, (128, 512), 1) + (q % 2) * 512
                v = v * keep + jnp.where(rr == cc, mark, 0.0)
            hi, lo = split(v)
            chi[rows] = hi
            clo[rows] = lo

        @pl.loop(0, 4)
        def _(j):
            rows = pl.ds(pl.multiple_of(j * 256, 256), 256)
            a_hi, a_lo = zhi[slot, rows], zlo[slot, rows]
            b_hi = chi[...]
            acc = jnp.dot(a_hi, b_hi, preferred_element_type=F32)
            acc += jnp.dot(a_hi, clo[...], preferred_element_type=F32)
            acc += jnp.dot(a_lo, b_hi, preferred_element_type=F32)
            acc = acc.reshape(4, 2, 32, 512)
            if new:
                st[k, j] = acc
            else:
                st[k, j] = st[k, j] + acc

    def rs_core(k):
        rcopy(st.at[k, :, :, 1 - c], xc.at[k], rsend.at[5 * k], rrecv.at[5 * k], sibling, y).start()

    def rs_one(k):
        wait_recv(xc.at[k], rrecv.at[5 * k])

        @pl.loop(0, 16)
        def _(i):
            xc[k, i // 4, i % 4] = xc[k, i // 4, i % 4] + st[k, i // 4, i % 4, c]

        for d in (1, 3, 2):
            rcopy(xc.at[k, :, (x + d) % 4, :, pl.ds(0, 256)], bx.at[k, d - 1], rsend.at[5 * k + 1],
                  rrecv.at[5 * k + 1], row_of(z, x + d, c), y).start()
            rcopy(xc.at[k, (z + d) % 4, :, :, pl.ds(256, 256)], bz.at[k, d - 1], rsend.at[5 * k + 2],
                  rrecv.at[5 * k + 2], row_of(z + d, x, c), y).start()

    def rs_two(k):
        wait_recv(bx.at[k], rrecv.at[5 * k + 1])
        for i in range(4):
            bx[k, 0, i] = bx[k, 0, i] + bx[k, 1, i] + bx[k, 2, i] + xc[k, i, x, :, 0:256]
        for d in (1, 3, 2):
            rcopy(bx.at[k, 0, (z + d) % 4], cx.at[k, d - 1], rsend.at[5 * k + 3], rrecv.at[5 * k + 3],
                  row_of(z + d, x, c), y).start()
        wait_recv(bz.at[k], rrecv.at[5 * k + 2])
        for i in range(4):
            bz[k, 0, i] = bz[k, 0, i] + bz[k, 1, i] + bz[k, 2, i] + xc[k, z, i, :, 256:512]
        for d in (1, 3, 2):
            rcopy(bz.at[k, 0, (x + d) % 4], cz.at[k, d - 1], rsend.at[5 * k + 4], rrecv.at[5 * k + 4],
                  row_of(z, x + d, c), y).start()

    def rs_three(k):
        q = (y + k) % 4
        wait_recv(cx.at[k], rrecv.at[5 * k + 3])
        rt[q, :, 0:256] = bx[k, 0, z] + cx[k, 0] + cx[k, 1] + cx[k, 2]
        wait_recv(cz.at[k], rrecv.at[5 * k + 4])
        rt[q, :, 256:512] = bz[k, 0, x] + cz[k, 0] + cz[k, 1] + cz[k, 2]

    def rs_sent(k):
        wait_send(xc.at[k], rsend.at[5 * k])
        wait_send(bx.at[k], rsend.at[5 * k + 1])
        wait_send(bz.at[k], rsend.at[5 * k + 2])
        wait_send(cx.at[k], rsend.at[5 * k + 3])
        wait_send(cz.at[k], rsend.at[5 * k + 4])

    def blocks_in():
        for j in range(8):
            lanes = pl.ds(128 * j, 128)
            pltpu.make_async_copy(
                ufull.at[j // 2, pl.ds((j % 2) * 2, 2), :, :, lanes], dblk.at[j], local.at[5]).start()
            for i in range(4):
                m = 31 - 4 * j - i
                pltpu.make_async_copy(
                    ufull.at[m // 8, (m // 2) % 4, m % 2, :, pl.ds(1024, 128)], dblk.at[8 + j, i // 2, i % 2],
                    local.at[5]).start()
        pltpu.make_async_copy(dblk, dblk, local.at[5]).wait()

    def inverses(lo, hi):
        @pl.loop(lo, hi)
        def _(g):
            for i in range(4):
                dinv[g * 4 + i] = inverse_unit_lower(dblk[g * 4 + i].reshape(128, 128))

    u_copies = [
        pltpu.make_async_copy(ufull.at[:, :, :, :, pl.ds(0, 1024)], first.at[:, :, :, 0], local.at[6]),
        pltpu.make_async_copy(ufull.at[:, :, :, :, pl.ds(1152, 1024)], first.at[:, :, :, 1], local.at[7]),
    ]

    def row_block(j, slot, lanes):
        return first[j // 2, (j % 2) * 2:(j % 2) * 2 + 2, :, slot, :, 0:lanes].reshape(128, lanes)

    def row_block_zero(j):
        parts = []
        for i in range(4):
            m = 31 - 4 * j - i
            parts.append(first[m // 8, (m // 2) % 4, m % 2, 0, :, 128 * (8 - j):1024])
        return jnp.concatenate(parts, axis=0)

    def substitute(which, upper):
        for j in range(7, -1, -1):
            xj = dot_high(rhs[:, 128 * j:128 * j + 128], dinv[8 * which + j])
            sol[:, 1024 * which + 128 * j:1024 * which + 128 * j + 128] = xj
            if j:
                rhs[:, 0:128 * j] = rhs[:, 0:128 * j] - dot_high(xj, upper(j))

    def substitute_one():
        rhs[:, 0:512] = -rt[2]
        rhs[:, 512:1024] = -rt[3]
        u_copies[0].wait()
        substitute(0, lambda j: row_block(j, 0, 128 * j))

    def substitute_zero():
        rhs[:, 0:512] = -rt[0]
        rhs[:, 512:1024] = -rt[1]
        u_copies[1].wait()
        for j in range(8):
            rhs[...] = rhs[...] - dot_high(sol[:, 128 * j:128 * j + 128], row_block(j, 1, 1024))
        substitute(1, row_block_zero)

    U, Z = (1152, 2176, 0), (1024, 2048, 5)
    y_own[0].start()
    y_own[1].start()

    @pl.when(p == 1)
    def _():
        scatter(lane1, 0)

    @pl.when((p == 0) & (y < 2))
    def _():
        scatter(lane0, 1)

    first_sends(0, 6)

    load_state(0, 0, 0)
    load_panel(panel.at[0], 0)
    load_panel(panel.at[1], 1)
    for t in range(8):
        if t < 7:
            load_state((t + 1) // 4, (t + 1) % 4, (t + 1) % 2)
        transposed(t // 4, t % 4, t % 2)
    u_round_y()
    for i in (2, 3, 4, 5):
        y_own[i].start()
    first_sends(6, 10)
    first_own()
    product(0, 0, 0, True)
    product(0, 1, 1, False)
    rs_core(0)
    u_here()
    u_pack()
    gather_a(packed, ufull, *U)
    rs_one(0)
    first_sends(10, 15)
    gather_b(packed, ufull, *U)
    rs_two(0)
    first_sends(15, 21)

    y_own[0].wait_recv()
    y_own[2].wait_recv()
    y_fwd[0].start()
    load_panel(gath.at[3, 0], 0)
    y_own[1].wait_recv()
    y_own[3].wait_recv()
    y_fwd[1].start()
    load_panel(gath.at[1, 1], 1)
    product(3, 0, 0, True)
    product(1, 1, 1, True)
    rs_three(0)
    first_sends(21, 26)
    gather_c(ufull, *U)
    first_sends(26, 31)

    y_own[4].wait_recv()
    load_panel(gath.at[3, 1], 0)
    y_own[5].wait_recv()
    load_panel(gath.at[1, 0], 1)
    product(3, 1, 0, False)
    rs_core(3)
    product(1, 0, 1, False)
    rs_core(1)
    gather_end(ufull, 0)
    blocks_in()
    rs_one(3)
    rs_one(1)
    inverses(0, 2)
    rs_two(3)
    rs_two(1)
    first_here()
    reorder()
    for copy in u_copies:
        copy.start()
    pltpu.make_async_copy(second.at[p], out.at[:, my_rows], local.at[9]).start()
    second_sends(0, 5)
    inverses(2, 4)
    rs_three(3)
    rs_three(1)

    y_fwd[0].wait_recv()
    load_panel(gath.at[2, 0], 0)
    y_fwd[1].wait_recv()
    load_panel(gath.at[2, 1], 1)
    product(2, 0, 0, True)
    product(2, 1, 1, False)
    rs_core(2)
    second_sends(5, 9)
    rs_one(2)
    second_sends(9, 13)
    rs_two(2)
    second_sends(13, 17)
    rs_three(2)
    substitute_one()
    substitute_zero()
    gather_a(sol, solved, *Z)
    second_sends(17, 22)
    gather_b(sol, solved, *Z)
    second_sends(22, 31)
    gather_c(solved, *Z)
    gather_end(solved, 5)
    wait_recv(second.at[pl.ds(0, 31)], arecv.at[1])
    pltpu.make_async_copy(second.at[p], out.at[:, my_rows], local.at[9]).wait()

    for d in y_own + y_fwd:
        d.wait_send()

    @pl.when(p == 1)
    def _():
        scatter_done(0)

    @pl.when((p == 0) & (y < 2))
    def _():
        scatter_done(1)

    wait_send(upc.at[:, pl.ds(0, 1536)], usend.at[2])

    @pl.when(y < 2)
    def _():
        wait_send(upc.at[:, pl.ds(0, 1536)], usend.at[3])

    first_sent()
    wait_send(second.at[pl.ds(0, 31)], asend.at[1])
    for k in range(4):
        rs_sent(k)
    gather_sent(ufull, *U)
    gather_sent(solved, *Z)


def main_call(state, panel, pivots):
    any_spec = pl.BlockSpec(memory_space=pl.ANY)
    shape = jax.ShapeDtypeStruct
    outs = [
        shape((2, 1024, 1024), F32), shape((4, 4, 2, 32, 2048), F32),
        shape((4, 2, 1024, 512), F32), shape((4, 4, 2, 32, 2176), F32),
    ]
    vmem = [
        ((2, 256, 1024), F32), ((2, 1024, 1024), BF16), ((2, 1024, 1024), BF16), ((2, 1024, 512), F32),
        ((1024, 512), BF16), ((1024, 512), BF16), ((4, 4, 4, 2, 32, 512), F32), ((4, 4, 4, 32, 512), F32),
        ((4, 3, 4, 32, 256), F32), ((4, 3, 4, 32, 256), F32), ((4, 3, 32, 256), F32), ((4, 3, 32, 256), F32),
        ((4, 4, 2, 2, 32, 1024), F32), ((32, 2, 32, 1024), F32), ((32, 3072), F32), ((32, 2176), F32),
        ((16, 128, 128), F32),
        ((16, 2, 2, 32, 128), F32), ((4, 32, 512), F32), ((32, 2048), F32), ((32, 1024), F32),
    ]
    sems = [8, 8, 2, 2, 4, 4, 20, 20, 10, 10, 12]
    return pl.pallas_call(
        main_kernel,
        out_shape=outs,
        in_specs=[any_spec, any_spec, pl.BlockSpec(memory_space=pltpu.SMEM)],
        out_specs=[any_spec] * 4,
        scratch_shapes=[pltpu.VMEM(*v) for v in vmem] + [DMA((n,)) for n in sems],
        compiler_params=pltpu.CompilerParams(
            collective_id=0, has_side_effects=True, vmem_limit_bytes=60 << 20),
    )(state, panel, pivots)


def select_kernel(ids, moved, one, zero, out):
    block = ids[pl.program_id(0)]

    @pl.when(block >= 2)
    def _():
        out[0] = moved[0]

    @pl.when(block == 1)
    def _():
        out[0] = one[...].T

    @pl.when(block == 0)
    def _():
        out[0] = zero[...].T


def select_call(ids, moved, solved):
    tile = 256
    tiles = 1024 // tile

    def rows_of(which):
        return pl.BlockSpec(
            (1024, tile), lambda l, i, ids: (0, (1 - which) * tiles + jnp.where(ids[l] == which, i, 0)))

    return pl.pallas_call(
        select_kernel,
        out_shape=jax.ShapeDtypeStruct((2, 1024, 1024), F32),
        grid_spec=pltpu.PrefetchScalarGridSpec(
            num_scalar_prefetch=1, grid=(2, tiles),
            in_specs=[pl.BlockSpec((1, tile, 1024), lambda l, i, ids: (l, i, 0)), rows_of(1), rows_of(0)],
            out_specs=pl.BlockSpec((1, tile, 1024), lambda l, i, ids: (l, i, 0))),
    )(ids, moved, solved, solved)


def body(state, panel, pivots):
    ids = lax.dynamic_slice(pivots.reshape(2, 32), (0, lax.axis_index("row")), (2, 1)).reshape(2)
    moved, solved, _, _ = main_call(state, panel, pivots)
    return select_call(ids, moved, solved.reshape(1024, 2048))


def solution(mesh):
    placed = (P(None, "row", "col"), P(None, "row", "col"), P())
    return jax.shard_map(
        body, mesh=mesh, in_specs=placed, out_specs=P(None, "row", "col"), check_vma=False)
```

```python
import functools

import jax
import jax.numpy as jnp
from jax import lax
from jax.experimental import pallas as pl
from jax.experimental.pallas import tpu as pltpu
from jax.sharding import PartitionSpec as P

MESH = pl.DeviceIdType.MESH
F32 = jnp.float32
BF16 = jnp.bfloat16
DMA = pltpu.SemaphoreType.DMA

ORDER = (20, 21, 1, 12, 24, 13, 25, 18, 6, 19, 7, 22, 2, 23, 3, 28, 8, 29, 9, 4, 16, 5, 17, 10, 30, 11, 31, 14, 26, 15, 27)


def split(v):
    hi = v.astype(BF16)
    return hi, (v - hi.astype(F32)).astype(BF16)


def dot_high(a, b):
    return jnp.dot(a, b, precision=lax.Precision.HIGHEST, preferred_element_type=F32)


def inverse_unit_lower(low):
    rows = lax.broadcasted_iota(jnp.int32, (128, 128), 0)
    cols = lax.broadcasted_iota(jnp.int32, (128, 128), 1)

    def part(s):
        keep = (rows // (2 * s) == cols // (2 * s)) & ((rows // s) % 2 == 1) & ((cols // s) % 2 == 0)
        return jnp.where(keep, low, 0.0)

    inv = jnp.where(rows == cols, 1.0, 0.0) - part(1)
    for s in (2, 4, 8, 16, 32, 64):
        inv = inv - dot_high(dot_high(inv, part(s)), inv)
    return inv


def main_kernel(
    state, panel, piv, out, solved, gath, ufull,
    zst, zhi, zlo, cst, chi, clo, st, xc, bx, bz, cx, cz, first, second, upc, packed, dinv, dblk, rt, sol, rhs,
    ysend, yrecv, asend, arecv, usend, urecv, rsend, rrecv, gsend, grecv, local,
):
    p = lax.axis_index("row")
    y = lax.axis_index("col")
    z, x, c = p // 8, (p // 2) % 4, p % 2

    def row_of(zz, xx, cc):
        return ((zz % 4) * 4 + xx % 4) * 2 + cc

    def peer(k):
        return row_of(z + k // 8, x + (k // 2) % 4, (c + k % 2) % 2)

    sibling = row_of(z, x, 1 - c)

    def rcopy(src, dst, ss, rs, row, col):
        return pltpu.make_async_remote_copy(src, dst, ss, rs, device_id=(row, col), device_id_type=MESH)

    def wait_recv(ref, rs):
        rcopy(ref, ref, rs, rs, sibling, y).wait_recv()

    def wait_send(ref, ss):
        rcopy(ref, ref, ss, ss, sibling, y).wait_send()

    right, left, across = (y + 1) % 4, (y + 3) % 4, (y + 2) % 4

    barrier = pltpu.get_barrier_semaphore()
    for k in range(1, 32):
        pl.semaphore_signal(barrier, inc=1, device_id=(peer(k), y), device_id_type=MESH)
    for d in (right, left, across):
        pl.semaphore_signal(barrier, inc=1, device_id=(p, d), device_id_type=MESH)
    pl.semaphore_wait(barrier, 34)

    top, bottom = pl.ds(0, 512), pl.ds(512, 512)
    y_own = [
        rcopy(panel.at[0, top], gath.at[3, 0, top], ysend.at[0], yrecv.at[0], p, right),
        rcopy(panel.at[1, top], gath.at[1, 1, top], ysend.at[1], yrecv.at[1], p, left),
        rcopy(panel.at[0, bottom], gath.at[3, 0, bottom], ysend.at[2], yrecv.at[2], p, right),
        rcopy(panel.at[1, bottom], gath.at[1, 1, bottom], ysend.at[3], yrecv.at[3], p, left),
        rcopy(panel.at[1], gath.at[3, 1], ysend.at[4], yrecv.at[4], p, right),
        rcopy(panel.at[0], gath.at[1, 0], ysend.at[5], yrecv.at[5], p, left),
    ]
    y_fwd = [
        rcopy(gath.at[3, 0], gath.at[2, 0], ysend.at[6], yrecv.at[6], p, right),
        rcopy(gath.at[1, 1], gath.at[2, 1], ysend.at[7], yrecv.at[7], p, left),
    ]

    lane1 = pl.ds(pl.multiple_of(y * 512, 512), 512)
    lane0 = pl.ds(pl.multiple_of(2048 + (y % 2) * 512, 512), 512)

    def scatter(lanes, sem):
        def rows_for(q):
            return pl.ds(pl.multiple_of((q if sem == 0 else 31 - q) * 32, 32), 32)

        for k in ORDER:
            q = peer(k)
            rcopy(panel.at[0, rows_for(q)], upc.at[:, lanes], usend.at[sem], urecv.at[sem], q, y).start()
        pltpu.make_async_copy(panel.at[0, rows_for(p)], upc.at[:, lanes], urecv.at[sem]).start()

    def scatter_done(sem):
        wait_send(panel.at[0, pl.ds(0, 31 * 32)], usend.at[sem])

    def u_round_y():
        wait_recv(upc.at[:, pl.ds(0, 512)], urecv.at[0])
        for d in (right, left, across):
            rcopy(upc.at[:, lane1], upc.at[:, lane1], usend.at[2], urecv.at[2], p, d).start()

        @pl.when(y < 2)
        def _():
            wait_recv(upc.at[:, pl.ds(0, 512)], urecv.at[1])
            for d in (right, left, across):
                rcopy(upc.at[:, lane0], upc.at[:, lane0], usend.at[3], urecv.at[3], p, d).start()

    def u_here():
        wait_recv(upc.at[:, pl.ds(0, 1536)], urecv.at[2])

        @pl.when(y < 2)
        def _():
            wait_recv(upc.at[:, pl.ds(0, 512)], urecv.at[3])

        @pl.when(y >= 2)
        def _():
            wait_recv(upc.at[:, pl.ds(0, 1024)], urecv.at[3])

    def u_pack():
        g = p // 4
        for t in range(9):
            lane = jnp.where(t <= g, 1024 + 128 * t, 2048 + 128 * (t - g - 1))
            packed[:, 128 * t:128 * t + 128] = upc[:, pl.ds(pl.multiple_of(lane, 128), 128)]
        packed[:, 1152:2176] = upc[:, 0:1024]

    def gather_a(share, full, h, w, base):
        pltpu.make_async_copy(share, full.at[z, x, c], local.at[10 + base // 5]).start()
        for d in (1, 3, 2):
            rcopy(share.at[:, pl.ds(0, h)], full.at[z, x, c, :, pl.ds(0, h)], gsend.at[base], grecv.at[base],
                  row_of(z, x + d, c), y).start()
            rcopy(share.at[:, pl.ds(h, w - h)], full.at[z, x, c, :, pl.ds(h, w - h)], gsend.at[base + 1],
                  grecv.at[base + 1], row_of(z + d, x, c), y).start()

    def gather_b(share, full, h, w, base):
        pltpu.make_async_copy(share, full.at[z, x, c], local.at[10 + base // 5]).wait()
        wait_recv(full.at[0, pl.ds(0, 3), 0, :, pl.ds(0, h)], grecv.at[base])
        for d in (1, 3, 2):
            here = full.at[z, :, c, :, pl.ds(0, h)]
            rcopy(here, here, gsend.at[base + 2], grecv.at[base + 2], row_of(z + d, x, c), y).start()
        wait_recv(full.at[0, pl.ds(0, 3), 0, :, pl.ds(h, w - h)], grecv.at[base + 1])
        for d in (1, 3, 2):
            here = full.at[:, x, c, :, pl.ds(h, w - h)]
            rcopy(here, here, gsend.at[base + 3], grecv.at[base + 3], row_of(z, x + d, c), y).start()

    def gather_c(full, h, w, base):
        wait_recv(full.at[pl.ds(0, 3), :, 0, :, pl.ds(0, h)], grecv.at[base + 2])
        wait_recv(full.at[pl.ds(0, 3), :, 0, :, pl.ds(h, w - h)], grecv.at[base + 3])
        rcopy(full.at[:, :, c], full.at[:, :, c], gsend.at[base + 4], grecv.at[base + 4], sibling, y).start()

    def gather_end(full, base):
        wait_recv(full.at[:, :, 0], grecv.at[base + 4])

    def gather_sent(full, h, w, base):
        wait_send(full.at[0, pl.ds(0, 3), 0, :, pl.ds(0, h)], gsend.at[base])
        wait_send(full.at[0, pl.ds(0, 3), 0, :, pl.ds(h, w - h)], gsend.at[base + 1])
        wait_send(full.at[pl.ds(0, 3), :, 0, :, pl.ds(0, h)], gsend.at[base + 2])
        wait_send(full.at[pl.ds(0, 3), :, 0, :, pl.ds(h, w - h)], gsend.at[base + 3])
        wait_send(full.at[:, :, 0], gsend.at[base + 4])

    def rows_of(q):
        return pl.ds(pl.multiple_of(q * 32, 32), 32)

    def first_sends(lo, hi):
        @pl.when(p >= 2)
        def _():
            for k in ORDER[lo:hi]:
                q = peer(k)
                rcopy(state.at[:, rows_of(q)], first.at[z, x, c], asend.at[0], arecv.at[0], q, y).start()

        @pl.when(p < 2)
        def _():
            for k in ORDER[lo:hi]:
                q = peer(k)
                rcopy(state.at[1, rows_of(q)], first.at[z, x, c, 1], asend.at[0], arecv.at[0], q, y).start()

    def first_own():
        first[0, 0, 0, 0] = jnp.zeros((32, 1024), F32)
        first[0, 0, 1, 0] = jnp.zeros((32, 1024), F32)

        @pl.when(p >= 2)
        def _():
            pltpu.make_async_copy(state.at[0, rows_of(p)], first.at[z, x, c, 0], local.at[9]).start()
            pltpu.make_async_copy(state.at[0, rows_of(p)], first.at[z, x, c, 0], local.at[9]).wait()

        pltpu.make_async_copy(state.at[1, rows_of(p)], first.at[z, x, c, 1], local.at[9]).start()
        pltpu.make_async_copy(state.at[1, rows_of(p)], first.at[z, x, c, 1], local.at[9]).wait()

    def first_here():
        @pl.when(p >= 2)
        def _():
            wait_recv(second.at[pl.ds(0, 30)], arecv.at[0])

        @pl.when(p < 2)
        def _():
            wait_recv(state.at[:, pl.ds(0, 976)], arecv.at[0])

    def first_sent():
        @pl.when(p >= 2)
        def _():
            wait_send(second.at[pl.ds(0, 31)], asend.at[0])

        @pl.when(p < 2)
        def _():
            wait_send(state.at[0, pl.ds(0, 992)], asend.at[0])

    my_rows = pl.ds(pl.multiple_of(p * 32, 32), 32)

    def second_sends(lo, hi):
        for k in ORDER[lo:hi]:
            q = peer(k)
            rcopy(second.at[q], out.at[:, my_rows], asend.at[1], arecv.at[1], q, y).start()

    def reorder():
        @pl.loop(0, 32)
        def _(q):
            for slot in range(2):
                b = piv[slot * 32 + q]
                owner = b % 32
                second[q, slot] = first[owner // 8, (owner // 2) % 4, owner % 2, b // 32]

    def transposed(slot, part, buf):
        pltpu.make_async_copy(
            state.at[slot, pl.ds(part * 256, 256)], zst.at[buf], local.at[buf]).wait()
        transposed_body(slot, part, buf)

    def transposed_body(slot, part, buf):
        @pl.loop(0, 4)
        def _(j):
            rows = pl.ds(pl.multiple_of(j * 256, 256), 256)
            hi, lo = split(zst[buf, :, rows].T)
            zhi[slot, rows, part * 256:part * 256 + 256] = hi
            zlo[slot, rows, part * 256:part * 256 + 256] = lo

    def load_state(slot, part, buf):
        pltpu.make_async_copy(
            state.at[slot, pl.ds(part * 256, 256)], zst.at[buf], local.at[buf]).start()

    def load_panel(src, buf):
        pltpu.make_async_copy(src, cst.at[buf], local.at[3 + buf]).start()

    keep = jnp.where(p >= 2, 1.0, 0.0).astype(F32)

    def product(k, slot, buf, new):
        pltpu.make_async_copy(panel.at[0], cst.at[buf], local.at[3 + buf]).wait()
        product_body(k, slot, buf, new)

    def product_body(k, slot, buf, new):
        q = (y + k) % 4
        mark = jnp.where(((p == 0) & (q < 2)) | ((p == 1) & (q >= 2)), -1.0, 0.0).astype(F32)

        @pl.loop(0, 8)
        def _(i):
            rows = pl.ds(pl.multiple_of(i * 128, 128), 128)
            v = cst[buf, rows]
            if slot == 0:
                rr = lax.broadcasted_iota(jnp.int32, (128, 512), 0) + i * 128
                cc = lax.broadcasted_iota(jnp.int32, (128, 512), 1) + (q % 2) * 512
                v = v * keep + jnp.where(rr == cc, mark, 0.0)
            hi, lo = split(v)
            chi[rows] = hi
            clo[rows] = lo

        @pl.loop(0, 4)
        def _(j):
            rows = pl.ds(pl.multiple_of(j * 256, 256), 256)
            a_hi, a_lo = zhi[slot, rows], zlo[slot, rows]
            b_hi = chi[...]
            acc = jnp.dot(a_hi, b_hi, preferred_element_type=F32)
            acc += jnp.dot(a_hi, clo[...], preferred_element_type=F32)
            acc += jnp.dot(a_lo, b_hi, preferred_element_type=F32)
            acc = acc.reshape(4, 2, 32, 512)
            if new:
                st[k, j] = acc
            else:
                st[k, j] = st[k, j] + acc

    def rs_core(k):
        rcopy(st.at[k, :, :, 1 - c], xc.at[k], rsend.at[5 * k], rrecv.at[5 * k], sibling, y).start()

    def rs_one(k):
        wait_recv(xc.at[k], rrecv.at[5 * k])

        @pl.loop(0, 16)
        def _(i):
            xc[k, i // 4, i % 4] = xc[k, i // 4, i % 4] + st[k, i // 4, i % 4, c]

        for d in (1, 3, 2):
            rcopy(xc.at[k, :, (x + d) % 4, :, pl.ds(0, 256)], bx.at[k, d - 1], rsend.at[5 * k + 1],
                  rrecv.at[5 * k + 1], row_of(z, x + d, c), y).start()
            rcopy(xc.at[k, (z + d) % 4, :, :, pl.ds(256, 256)], bz.at[k, d - 1], rsend.at[5 * k + 2],
                  rrecv.at[5 * k + 2], row_of(z + d, x, c), y).start()

    def rs_two(k):
        wait_recv(bx.at[k], rrecv.at[5 * k + 1])
        for i in range(4):
            bx[k, 0, i] = bx[k, 0, i] + bx[k, 1, i] + bx[k, 2, i] + xc[k, i, x, :, 0:256]
        for d in (1, 3, 2):
            rcopy(bx.at[k, 0, (z + d) % 4], cx.at[k, d - 1], rsend.at[5 * k + 3], rrecv.at[5 * k + 3],
                  row_of(z + d, x, c), y).start()
        wait_recv(bz.at[k], rrecv.at[5 * k + 2])
        for i in range(4):
            bz[k, 0, i] = bz[k, 0, i] + bz[k, 1, i] + bz[k, 2, i] + xc[k, z, i, :, 256:512]
        for d in (1, 3, 2):
            rcopy(bz.at[k, 0, (x + d) % 4], cz.at[k, d - 1], rsend.at[5 * k + 4], rrecv.at[5 * k + 4],
                  row_of(z, x + d, c), y).start()

    def rs_three(k):
        q = (y + k) % 4
        wait_recv(cx.at[k], rrecv.at[5 * k + 3])
        rt[q, :, 0:256] = bx[k, 0, z] + cx[k, 0] + cx[k, 1] + cx[k, 2]
        wait_recv(cz.at[k], rrecv.at[5 * k + 4])
        rt[q, :, 256:512] = bz[k, 0, x] + cz[k, 0] + cz[k, 1] + cz[k, 2]

    def rs_sent(k):
        wait_send(xc.at[k], rsend.at[5 * k])
        wait_send(bx.at[k], rsend.at[5 * k + 1])
        wait_send(bz.at[k], rsend.at[5 * k + 2])
        wait_send(cx.at[k], rsend.at[5 * k + 3])
        wait_send(cz.at[k], rsend.at[5 * k + 4])

    def blocks_in():
        for j in range(8):
            lanes = pl.ds(128 * j, 128)
            pltpu.make_async_copy(
                ufull.at[j // 2, pl.ds((j % 2) * 2, 2), :, :, lanes], dblk.at[j], local.at[5]).start()
            for i in range(4):
                m = 31 - 4 * j - i
                pltpu.make_async_copy(
                    ufull.at[m // 8, (m // 2) % 4, m % 2, :, pl.ds(1024, 128)], dblk.at[8 + j, i // 2, i % 2],
                    local.at[5]).start()
        pltpu.make_async_copy(dblk, dblk, local.at[5]).wait()

    def inverses(lo, hi):
        @pl.loop(lo, hi)
        def _(g):
            for i in range(4):
                dinv[g * 4 + i] = inverse_unit_lower(dblk[g * 4 + i].reshape(128, 128))

    u_copies = [
        pltpu.make_async_copy(ufull.at[:, :, :, :, pl.ds(0, 1024)], first.at[:, :, :, 0], local.at[6]),
        pltpu.make_async_copy(ufull.at[:, :, :, :, pl.ds(1152, 1024)], first.at[:, :, :, 1], local.at[7]),
    ]

    def row_block(j, slot, lanes):
        return first[j // 2, (j % 2) * 2:(j % 2) * 2 + 2, :, slot, :, 0:lanes].reshape(128, lanes)

    def row_block_zero(j):
        parts = []
        for i in range(4):
            m = 31 - 4 * j - i
            parts.append(first[m // 8, (m // 2) % 4, m % 2, 0, :, 128 * (8 - j):1024])
        return jnp.concatenate(parts, axis=0)

    def substitute(which, upper):
        for j in range(7, -1, -1):
            xj = dot_high(rhs[:, 128 * j:128 * j + 128], dinv[8 * which + j])
            sol[:, 1024 * which + 128 * j:1024 * which + 128 * j + 128] = xj
            if j:
                rhs[:, 0:128 * j] = rhs[:, 0:128 * j] - dot_high(xj, upper(j))

    def substitute_one():
        rhs[:, 0:512] = -rt[2]
        rhs[:, 512:1024] = -rt[3]
        u_copies[0].wait()
        substitute(0, lambda j: row_block(j, 0, 128 * j))

    def substitute_zero():
        rhs[:, 0:512] = -rt[0]
        rhs[:, 512:1024] = -rt[1]
        u_copies[1].wait()
        for j in range(8):
            rhs[...] = rhs[...] - dot_high(sol[:, 128 * j:128 * j + 128], row_block(j, 1, 1024))
        substitute(1, row_block_zero)

    U, Z = (1152, 2176, 0), (1024, 2048, 5)
    y_own[0].start()
    y_own[1].start()

    @pl.when(p == 1)
    def _():
        scatter(lane1, 0)

    @pl.when((p == 0) & (y < 2))
    def _():
        scatter(lane0, 1)

    first_sends(0, 6)

    load_state(0, 0, 0)
    load_panel(panel.at[0], 0)
    load_panel(panel.at[1], 1)
    for t in range(8):
        if t < 7:
            load_state((t + 1) // 4, (t + 1) % 4, (t + 1) % 2)
        transposed(t // 4, t % 4, t % 2)
    u_round_y()
    for i in (2, 3, 4, 5):
        y_own[i].start()
    first_sends(6, 10)
    first_own()
    product(0, 0, 0, True)
    product(0, 1, 1, False)
    rs_core(0)
    u_here()
    u_pack()
    gather_a(packed, ufull, *U)
    rs_one(0)
    first_sends(10, 15)
    gather_b(packed, ufull, *U)
    rs_two(0)
    first_sends(15, 21)

    y_own[0].wait_recv()
    y_own[2].wait_recv()
    y_fwd[0].start()
    load_panel(gath.at[3, 0], 0)
    y_own[1].wait_recv()
    y_own[3].wait_recv()
    y_fwd[1].start()
    load_panel(gath.at[1, 1], 1)
    product(3, 0, 0, True)
    product(1, 1, 1, True)
    rs_three(0)
    first_sends(21, 26)
    gather_c(ufull, *U)
    first_sends(26, 31)

    y_own[4].wait_recv()
    load_panel(gath.at[3, 1], 0)
    y_own[5].wait_recv()
    load_panel(gath.at[1, 0], 1)
    product(3, 1, 0, False)
    rs_core(3)
    product(1, 0, 1, False)
    rs_core(1)
    gather_end(ufull, 0)
    blocks_in()
    rs_one(3)
    rs_one(1)
    inverses(0, 2)
    rs_two(3)
    rs_two(1)
    first_here()
    reorder()
    for copy in u_copies:
        copy.start()
    pltpu.make_async_copy(second.at[p], out.at[:, my_rows], local.at[9]).start()
    second_sends(0, 5)
    inverses(2, 4)
    rs_three(3)
    rs_three(1)

    y_fwd[0].wait_recv()
    load_panel(gath.at[2, 0], 0)
    y_fwd[1].wait_recv()
    load_panel(gath.at[2, 1], 1)
    product(2, 0, 0, True)
    product(2, 1, 1, False)
    rs_core(2)
    second_sends(5, 9)
    rs_one(2)
    second_sends(9, 13)
    rs_two(2)
    second_sends(13, 17)
    rs_three(2)
    substitute_one()
    substitute_zero()
    gather_a(sol, solved, *Z)
    second_sends(17, 22)
    gather_b(sol, solved, *Z)
    second_sends(22, 31)
    gather_c(solved, *Z)
    gather_end(solved, 5)
    wait_recv(second.at[pl.ds(0, 31)], arecv.at[1])
    pltpu.make_async_copy(second.at[p], out.at[:, my_rows], local.at[9]).wait()

    for d in y_own + y_fwd:
        d.wait_send()

    @pl.when(p == 1)
    def _():
        scatter_done(0)

    @pl.when((p == 0) & (y < 2))
    def _():
        scatter_done(1)

    wait_send(upc.at[:, pl.ds(0, 1536)], usend.at[2])

    @pl.when(y < 2)
    def _():
        wait_send(upc.at[:, pl.ds(0, 1536)], usend.at[3])

    first_sent()
    wait_send(second.at[pl.ds(0, 31)], asend.at[1])
    for k in range(4):
        rs_sent(k)
    gather_sent(ufull, *U)
    gather_sent(solved, *Z)


def main_call(state, panel, pivots):
    any_spec = pl.BlockSpec(memory_space=pl.ANY)
    shape = jax.ShapeDtypeStruct
    outs = [
        shape((2, 1024, 1024), F32), shape((4, 4, 2, 32, 2048), F32),
        shape((4, 2, 1024, 512), F32), shape((4, 4, 2, 32, 2176), F32),
    ]
    vmem = [
        ((2, 256, 1024), F32), ((2, 1024, 1024), BF16), ((2, 1024, 1024), BF16), ((2, 1024, 512), F32),
        ((1024, 512), BF16), ((1024, 512), BF16), ((4, 4, 4, 2, 32, 512), F32), ((4, 4, 4, 32, 512), F32),
        ((4, 3, 4, 32, 256), F32), ((4, 3, 4, 32, 256), F32), ((4, 3, 32, 256), F32), ((4, 3, 32, 256), F32),
        ((4, 4, 2, 2, 32, 1024), F32), ((32, 2, 32, 1024), F32), ((32, 3072), F32), ((32, 2176), F32),
        ((16, 128, 128), F32),
        ((16, 2, 2, 32, 128), F32), ((4, 32, 512), F32), ((32, 2048), F32), ((32, 1024), F32),
    ]
    sems = [8, 8, 2, 2, 4, 4, 20, 20, 10, 10, 12]
    return pl.pallas_call(
        main_kernel,
        out_shape=outs,
        in_specs=[any_spec, any_spec, pl.BlockSpec(memory_space=pltpu.SMEM)],
        out_specs=[any_spec] * 4,
        scratch_shapes=[pltpu.VMEM(*v) for v in vmem] + [DMA((n,)) for n in sems],
        compiler_params=pltpu.CompilerParams(
            collective_id=0, has_side_effects=True, vmem_limit_bytes=60 << 20),
    )(state, panel, pivots)


def select_kernel(ids, moved, solved, out):
    block = ids[pl.program_id(0)]

    @pl.when(block >= 2)
    def _():
        out[0] = moved[0]

    @pl.when(block < 2)
    def _():
        out[0] = solved[...].T


def select_call(ids, moved, solved):
    tile = 256
    tiles = 1024 // tile

    def solved_tile(l, i, ids):
        return 0, jnp.where(ids[l] < 2, (1 - ids[l]) * tiles + i, 0)

    return pl.pallas_call(
        select_kernel,
        out_shape=jax.ShapeDtypeStruct((2, 1024, 1024), F32),
        grid_spec=pltpu.PrefetchScalarGridSpec(
            num_scalar_prefetch=1, grid=(2, tiles),
            in_specs=[pl.BlockSpec((1, tile, 1024), lambda l, i, ids: (l, i, 0)),
                      pl.BlockSpec((1024, tile), solved_tile)],
            out_specs=pl.BlockSpec((1, tile, 1024), lambda l, i, ids: (l, i, 0))),
    )(ids, moved, solved)


def body(state, panel, pivots):
    ids = lax.dynamic_slice(pivots.reshape(2, 32), (0, lax.axis_index("row")), (2, 1)).reshape(2)
    moved, solved, _, _ = main_call(state, panel, pivots)
    return select_call(ids, moved, solved.reshape(1024, 2048))


def solution(mesh):
    placed = (P(None, "row", "col"), P(None, "row", "col"), P())
    return jax.shard_map(
        body, mesh=mesh, in_specs=placed, out_specs=P(None, "row", "col"), check_vma=False)
```
